512 devices in a mesh: pipe: 16 (over y, z_lo), dp: 32 (over z_hi, x, core).
Axes of the slice: x: 4, y: 4, z: 16 (z_hi: 4, z_lo: 4; z = z_hi * 4 + z_lo), core: 2. Of those that a mesh axis runs over, the one named last changes fastest.
Arguments:
- grad_out: bfloat16 [16, 2, 2, 128, 3584], P('pipe', None, None, 'dp'), may hold values from -6 to 6
- hidden: bfloat16 [16, 2, 2, 128, 9216], P('pipe', None, None, None, 'dp'), may hold values from -5 to 5
- weights: bfloat16 [16, 9216, 3584], P('pipe', 'dp'), may hold values from -5 to 5
- counts: int32 [16, 2, 2, 32], P('pipe', None, None, 'dp'), may hold values from 1 to 4
Outputs:
- grad_hidden: bfloat16 [16, 2, 2, 128, 9216], P('pipe', None, None, None, 'dp')
- new_weights: bfloat16 [16, 9216, 3584], P('pipe', 'dp')
The draws below stay inside these ranges and needn't reach their ends.
All inputs are finite; a program needn't handle non-finite values.
Results may differ from the reference program's by a relative error of at most 0.0034.
Values may be sent and summed in bfloat16 or wider, within the bound.
No kernel may reach another device: no remote copies, remote signals or barrier semaphores. Data moves between devices by JAX's collectives and lax.ppermute only.
A program may use at most 64 MiB of HBM per device.

```python
import jax
import jax.numpy as jnp
from jax import lax

D = 3584
H = 9216
M = 2
ROWS = 4
TOKROWS = 128
N_PIPE = 16
N_DP = 32


def with_ends(array, key, least, high):
    index_at = [jax.random.randint(jax.random.fold_in(key, axis), (), 0, length) for axis, length in enumerate(array.shape)]
    widest = array.shape.index(max(array.shape))
    neighbour = index_at[:widest] + [(index_at[widest] + 1) % array.shape[widest]] + index_at[widest + 1:]
    return array.at[tuple(index_at)].set(least).at[tuple(neighbour)].set(high)


def block_levels(rng, dims, pieces, smallest, high):
    def one(axis_at, blocks):
        draws = jax.random.uniform(jax.random.fold_in(jax.random.fold_in(rng, 6), axis_at), (blocks,), jnp.float32, smallest / len(pieces), high / len(pieces))
        return jnp.repeat(jnp.exp(draws), dims[axis_at] // blocks).reshape((-1,) + (1,) * (len(dims) - axis_at - 1))

    loudness = one(*pieces[0])
    for cut in pieces[1:]:
        loudness = loudness * one(*cut)
    return loudness


def bell_draw(key, extent, width, limit, pieces=(), held_as=jnp.bfloat16):
    drawn = width * jax.random.normal(key, extent, jnp.float32)
    if pieces:
        drawn = drawn * block_levels(key, extent, pieces, -0.22, 0.18)
    return jnp.clip(drawn, -limit, limit).astype(held_as)


def setup_inputs(seed: int = 0) -> dict:
    key_list = jax.random.split(jax.random.key(seed), 5)
    return {
        "grad_out": bell_draw(key_list[0], (N_PIPE, 2, M, TOKROWS, D), 1.0, 6.0, ((0, 16), (3, 32))),
        "hidden": bell_draw(key_list[1], (N_PIPE, 2, M, TOKROWS, H), 1.0, 5.0, ((0, 16), (4, 32))),
        "weights": bell_draw(key_list[2], (N_PIPE, H, D), 1.0, 5.0, ((0, 16), (1, 32))),
        "counts": with_ends(jax.random.randint(key_list[3], (N_PIPE, 2, M, N_DP), 1, ROWS + 1), jax.random.fold_in(key_list[3], 1), 1, ROWS).astype(jnp.int32),
    }


step_rate = 2.0


def reference(grad_out, hidden, weights, counts):
    scale_factor = D ** -0.5
    slot_index = jnp.arange(ROWS * N_DP, dtype=jnp.int32) % ROWS
    live_rows = jnp.repeat(counts, ROWS, axis=3) > slot_index
    masked = jnp.where(live_rows[..., None], grad_out, jnp.zeros_like(grad_out))
    section_rows = jnp.stack([masked[:, 0], masked[::-1, 1]], axis=1)
    section_acts = jnp.stack([hidden[:, 0], hidden[::-1, 1]], axis=1)

    def one_section(items):
        rows, acts, section_weight = items
        rows_f32 = rows.astype(jnp.float32)
        weight_f32 = section_weight.astype(jnp.float32)
        grad_rows = (jnp.einsum("rmtd,hd->rmth", rows_f32, weight_f32) * scale_factor).astype(jnp.bfloat16)
        partial_value = (jnp.einsum("rmth,rmtd->rhd", acts.astype(jnp.float32), rows_f32) * scale_factor).astype(jnp.bfloat16)
        gradient = partial_value[0].astype(jnp.float32) + partial_value[1].astype(jnp.float32)
        return grad_rows, (weight_f32 - step_rate * gradient).astype(jnp.bfloat16)

    section_grads, new_weights = lax.map(one_section, (section_rows, section_acts, weights))
    grad_hidden = jnp.stack([section_grads[:, 0], section_grads[::-1, 1]], axis=1)
    return grad_hidden, new_weights
```

```python
import numpy as np

import jax
import jax.numpy as jnp
from jax import lax
from jax.sharding import Mesh
from jax.sharding import PartitionSpec as P

step_rate = 2.0

PIPE = ("py", "pz")
DP = ("dz", "dx", "dc")


def mirror(block):
    count = lax.axis_size(PIPE)
    route = [(low, count - 1 - low) for low in range(count)]
    return lax.ppermute(block, PIPE, route)


def gather_rows(block):
    lead = block.ndim - 2
    out = block
    out = lax.all_gather(out, "dz", axis=0)
    out = lax.all_gather(out, "dx", axis=1)
    out = lax.all_gather(out, "dc", axis=2)
    perm = tuple(range(3, 3 + lead)) + (0, 1, 2, 3 + lead, 4 + lead)
    out = jnp.transpose(out, perm)
    shape = out.shape
    return out.reshape(shape[:lead] + (-1, shape[-1]))


def shards(grad_out, hidden, weights, counts):
    row_total = grad_out.shape[3]
    full_width = grad_out.shape[4]
    scale_factor = float(full_width) ** (-0.5)
    slot_index = lax.broadcasted_iota(jnp.int32, (1, 1, 1, row_total), 3)
    live_rows = slot_index < counts
    masked = jnp.where(live_rows[..., None], grad_out, jnp.zeros_like(grad_out))
    own_weight = weights[0]
    mirror_masked, mirror_hidden = mirror((masked[0, 1], hidden[0, 1]))
    both_masked = jnp.stack([masked[0, 0], mirror_masked], axis=0)
    both_hidden = jnp.stack([hidden[0, 0], mirror_hidden], axis=0)
    piece = gather_rows(both_masked)
    grad_acc = jnp.einsum("rmkd,hd->rmkh", piece, own_weight, preferred_element_type=jnp.float32)
    weight_acc = jnp.einsum(
        "rmkh,rmkd->rhd", both_hidden, piece, preferred_element_type=jnp.float32
    )
    grad_rows = (grad_acc * scale_factor).astype(jnp.bfloat16)
    partial_value = (weight_acc * scale_factor).astype(jnp.bfloat16)
    gradient = partial_value[0].astype(jnp.float32) + partial_value[1].astype(jnp.float32)
    new_weight = (own_weight.astype(jnp.float32) - step_rate * gradient).astype(jnp.bfloat16)
    returned = mirror(grad_rows[1])
    grad_hidden = jnp.stack([grad_rows[0], returned], axis=0)[None]
    return (grad_hidden, new_weight[None])


def solution(mesh):
    n_pipe, n_dp = mesh.devices.shape
    fine = Mesh(mesh.devices.reshape(4, n_pipe // 4, 4, 4, n_dp // 16), PIPE + DP)
    return jax.shard_map(
        shards,
        mesh=fine,
        in_specs=(
            P(PIPE, None, None, DP, None),
            P(PIPE, None, None, None, DP),
            P(PIPE, DP, None),
            P(PIPE, None, None, DP),
        ),
        out_specs=(P(PIPE, None, None, None, DP), P(PIPE, DP, None)),
        check_vma=False,
    )
```

```python
import jax
import jax.numpy as jnp
from jax import lax
from jax.sharding import Mesh
from jax.sharding import PartitionSpec as P

step_rate = 2.0

PIPE = ("py", "pz")
DP = ("dz", "dx", "dc")


def mirror(block):
    count = lax.axis_size(PIPE)
    route = [(low, count - 1 - low) for low in range(count)]
    return lax.ppermute(block, PIPE, route)


def gather_rows(block):
    out = lax.all_gather(block, "dz", axis=0)
    out = lax.all_gather(out, "dx", axis=1)
    out = lax.all_gather(out, "dc", axis=2)
    return out.reshape(-1, block.shape[-1])


def one_slot(rows, acts, weight, scale_factor):
    micro, tok, width = rows.shape
    share = acts.shape[-1]
    piece = gather_rows(rows.reshape(micro * tok, width))
    ranks = piece.shape[0] // (micro * tok)
    grad = jnp.dot(piece, weight.T, preferred_element_type=jnp.float32)
    grad = (grad * scale_factor).astype(jnp.bfloat16)
    grad = grad.reshape(ranks, micro, tok, share).transpose(1, 0, 2, 3).reshape(micro, ranks * tok, share)
    acts_rows = acts.reshape(micro, ranks, tok, share).transpose(1, 0, 2, 3).reshape(ranks * micro * tok, share)
    part = jnp.dot(acts_rows.T, piece, preferred_element_type=jnp.float32)
    part = (part * scale_factor).astype(jnp.bfloat16)
    return grad, part


def shards(grad_out, hidden, weights, counts):
    row_total = grad_out.shape[3]
    full_width = grad_out.shape[4]
    scale_factor = float(full_width) ** (-0.5)
    slot_index = lax.broadcasted_iota(jnp.int32, (1, 1, 1, row_total), 3)
    live_rows = slot_index < counts
    masked = jnp.where(live_rows[..., None], grad_out, jnp.zeros_like(grad_out))
    own_weight = weights[0]
    mirror_masked, mirror_hidden = mirror((masked[0, 1], hidden[0, 1]))
    grad_own, part_own = one_slot(masked[0, 0], hidden[0, 0], own_weight, scale_factor)
    grad_mirror, part_mirror = one_slot(mirror_masked, mirror_hidden, own_weight, scale_factor)
    gradient = part_own.astype(jnp.float32) + part_mirror.astype(jnp.float32)
    new_weight = (own_weight.astype(jnp.float32) - step_rate * gradient).astype(jnp.bfloat16)
    returned = mirror(grad_mirror)
    grad_hidden = jnp.stack([grad_own, returned], axis=0)[None]
    return (grad_hidden, new_weight[None])


def solution(mesh):
    n_pipe, n_dp = mesh.devices.shape
    fine = Mesh(mesh.devices.reshape(4, n_pipe // 4, 4, 4, n_dp // 16), PIPE + DP)
    return jax.shard_map(
        shards,
        mesh=fine,
        in_specs=(
            P(PIPE, None, None, DP, None),
            P(PIPE, None, None, None, DP),
            P(PIPE, DP, None),
            P(PIPE, None, None, DP),
        ),
        out_specs=(P(PIPE, None, None, None, DP), P(PIPE, DP, None)),
        check_vma=False,
    )
```

```python
import jax
import jax.numpy as jnp
from jax import lax
from jax.sharding import Mesh
from jax.sharding import PartitionSpec as P

step_rate = 2.0

PIPE = ("py", "pz")
DP = ("dz", "dx", "dc")


def mirror(block):
    count = lax.axis_size(PIPE)
    route = [(low, count - 1 - low) for low in range(count)]
    return lax.ppermute(block, PIPE, route)


def gather_rows(block):
    out = lax.all_gather(block, "dz", axis=0)
    out = lax.all_gather(out, "dx", axis=1)
    out = lax.all_gather(out, "dc", axis=2)
    return out.reshape(-1, block.shape[-1])


def shards(grad_out, hidden, weights, counts):
    row_total = grad_out.shape[3]
    full_width = grad_out.shape[4]
    micro = grad_out.shape[2]
    tokens = hidden.shape[3]
    share = hidden.shape[4]
    scale_factor = float(full_width) ** (-0.5)
    slot_index = lax.broadcasted_iota(jnp.int32, (1, 1, 1, row_total), 3)
    live_rows = slot_index < counts
    masked = jnp.where(live_rows[..., None], grad_out, jnp.zeros_like(grad_out))
    own_weight = weights[0]
    mirror_masked, mirror_hidden = mirror((masked[0, 1], hidden[0, 1]))
    both_masked = jnp.stack([masked[0, 0], mirror_masked], axis=0)
    both_hidden = jnp.stack([hidden[0, 0], mirror_hidden], axis=0)
    piece = gather_rows(both_masked.reshape(-1, full_width))
    ranks = tokens // row_total
    acts = both_hidden.reshape(2, micro, ranks, row_total, share).transpose(2, 0, 1, 3, 4).reshape(-1, share)
    grad = jnp.dot(piece, own_weight.T, preferred_element_type=jnp.float32)
    grad = (grad * scale_factor).astype(jnp.bfloat16)
    grad = grad.reshape(ranks, 2, micro, row_total, share).transpose(1, 2, 0, 3, 4).reshape(2, micro, tokens, share)
    total = jnp.dot(acts.T, piece, preferred_element_type=jnp.float32)
    gradient = total * scale_factor
    new_weight = (own_weight.astype(jnp.float32) - step_rate * gradient).astype(jnp.bfloat16)
    returned = mirror(grad[1])
    grad_hidden = jnp.stack([grad[0], returned], axis=0)[None]
    return (grad_hidden, new_weight[None])


def solution(mesh):
    n_pipe, n_dp = mesh.devices.shape
    fine = Mesh(mesh.devices.reshape(4, n_pipe // 4, 4, 4, n_dp // 16), PIPE + DP)
    return jax.shard_map(
        shards,
        mesh=fine,
        in_specs=(
            P(PIPE, None, None, DP, None),
            P(PIPE, None, None, None, DP),
            P(PIPE, DP, None),
            P(PIPE, None, None, DP),
        ),
        out_specs=(P(PIPE, None, None, None, DP), P(PIPE, DP, None)),
        check_vma=False,
    )
```

```python
import jax
import jax.numpy as jnp
from jax import lax
from jax.sharding import Mesh
from jax.sharding import PartitionSpec as P

step_rate = 2.0

PIPE = ("py", "pz")
DP = ("dz", "dx", "dc")


def mirror(block):
    count = lax.axis_size(PIPE)
    route = [(low, count - 1 - low) for low in range(count)]
    return lax.ppermute(block, PIPE, route)


def gather_rows(block):
    out = lax.all_gather(block, "dz", axis=0)
    out = lax.all_gather(out, ("dx", "dc"), axis=1)
    return out.reshape(-1, block.shape[-1])


def shards(grad_out, hidden, weights, counts):
    row_total = grad_out.shape[3]
    full_width = grad_out.shape[4]
    micro = grad_out.shape[2]
    tokens = hidden.shape[3]
    share = hidden.shape[4]
    scale_factor = float(full_width) ** (-0.5)
    slot_index = lax.broadcasted_iota(jnp.int32, (1, 1, 1, row_total), 3)
    live_rows = slot_index < counts
    masked = jnp.where(live_rows[..., None], grad_out, jnp.zeros_like(grad_out))
    own_weight = weights[0]
    mirror_masked, mirror_hidden = mirror((masked[0, 1], hidden[0, 1]))
    both_masked = jnp.stack([masked[0, 0], mirror_masked], axis=0)
    both_hidden = jnp.stack([hidden[0, 0], mirror_hidden], axis=0)
    piece = gather_rows(both_masked.reshape(-1, full_width))
    ranks = tokens // row_total
    acts = both_hidden.reshape(2, micro, ranks, row_total, share).transpose(2, 0, 1, 3, 4).reshape(-1, share)
    grad = jnp.dot(piece, own_weight.T, preferred_element_type=jnp.float32)
    grad = (grad * scale_factor).astype(jnp.bfloat16)
    grad = grad.reshape(ranks, 2, micro, row_total, share).transpose(1, 2, 0, 3, 4).reshape(2, micro, tokens, share)
    total = jnp.dot(acts.T, piece, preferred_element_type=jnp.float32)
    gradient = total * scale_factor
    new_weight = (own_weight.astype(jnp.float32) - step_rate * gradient).astype(jnp.bfloat16)
    returned = mirror(grad[1])
    grad_hidden = jnp.stack([grad[0], returned], axis=0)[None]
    return (grad_hidden, new_weight[None])


def solution(mesh):
    n_pipe, n_dp = mesh.devices.shape
    fine = Mesh(mesh.devices.reshape(4, n_pipe // 4, 4, 4, n_dp // 16), PIPE + DP)
    return jax.shard_map(
        shards,
        mesh=fine,
        in_specs=(
            P(PIPE, None, None, DP, None),
            P(PIPE, None, None, None, DP),
            P(PIPE, DP, None),
            P(PIPE, None, None, DP),
        ),
        out_specs=(P(PIPE, None, None, None, DP), P(PIPE, DP, None)),
        check_vma=False,
    )
```

```python
import jax
import jax.numpy as jnp
from jax import lax
from jax.sharding import Mesh
from jax.sharding import PartitionSpec as P

step_rate = 2.0

PIPE = ("py", "pz")
DP = ("dz", "dx", "dc")


def mirror(block):
    count = lax.axis_size(PIPE)
    route = [(low, count - 1 - low) for low in range(count)]
    return lax.ppermute(block, PIPE, route)


def shards(grad_out, hidden, weights, counts):
    row_total = grad_out.shape[3]
    full_width = grad_out.shape[4]
    micro = grad_out.shape[2]
    tokens = hidden.shape[3]
    share = hidden.shape[4]
    ranks = tokens // row_total
    scale_factor = float(full_width) ** (-0.5)
    slot_index = lax.broadcasted_iota(jnp.int32, (1, 1, 1, row_total), 3)
    live_rows = slot_index < counts
    masked = jnp.where(live_rows[..., None], grad_out, jnp.zeros_like(grad_out))
    own_weight = weights[0]
    own_rows = lax.all_gather(masked[0].reshape(2, -1, full_width), "dz", axis=1)
    mirror_rows, mirror_hidden = mirror((own_rows[1], hidden[0, 1]))
    pieces = [lax.all_gather(own_rows[0], ("dx", "dc"), axis=1), lax.all_gather(mirror_rows, ("dx", "dc"), axis=1)]
    pieces = [piece.reshape(-1, full_width) for piece in pieces]
    grads = []
    total = None
    for piece, acts in zip(pieces, (hidden[0, 0], mirror_hidden)):
        grad = jnp.dot(piece, own_weight.T, preferred_element_type=jnp.float32)
        grad = (grad * scale_factor).astype(jnp.bfloat16)
        grads.append(grad.reshape(ranks, micro, row_total, share).transpose(1, 0, 2, 3).reshape(micro, tokens, share))
        rows = acts.reshape(micro, ranks, row_total, share).transpose(1, 0, 2, 3).reshape(-1, share)
        part = jnp.dot(rows.T, piece, preferred_element_type=jnp.float32)
        total = part if total is None else total + part
    gradient = total * scale_factor
    new_weight = (own_weight.astype(jnp.float32) - step_rate * gradient).astype(jnp.bfloat16)
    returned = mirror(grads[1])
    grad_hidden = jnp.stack([grads[0], returned], axis=0)[None]
    return (grad_hidden, new_weight[None])


def solution(mesh):
    n_pipe, n_dp = mesh.devices.shape
    fine = Mesh(mesh.devices.reshape(4, n_pipe // 4, 4, 4, n_dp // 16), PIPE + DP)
    return jax.shard_map(
        shards,
        mesh=fine,
        in_specs=(
            P(PIPE, None, None, DP, None),
            P(PIPE, None, None, None, DP),
            P(PIPE, DP, None),
            P(PIPE, None, None, DP),
        ),
        out_specs=(P(PIPE, None, None, None, DP), P(PIPE, DP, None)),
        check_vma=False,
    )
```

```python
import functools

import jax
import jax.numpy as jnp
from jax import lax
from jax.experimental import pallas as pl
from jax.experimental.pallas import tpu as pltpu
from jax.sharding import Mesh
from jax.sharding import PartitionSpec as P

step_rate = 2.0

PIPE = ("py", "pz")
DP = ("dz", "dx", "dc")


def mirror(block):
    count = lax.axis_size(PIPE)
    route = [(low, count - 1 - low) for low in range(count)]
    return lax.ppermute(block, PIPE, route)


def gather_rows(block):
    out = lax.all_gather(block, "dz", axis=0)
    out = lax.all_gather(out, ("dx", "dc"), axis=1)
    return out.reshape(-1, block.shape[-1])


def tail_kernel(piece_ref, w_ref, acts_ref, grad_ref, neww_ref, acc_ref, *, scale, rate):
    i = pl.program_id(0)

    @pl.when(i == 0)
    def _():
        acc_ref[...] = jnp.zeros_like(acc_ref)

    rows = piece_ref[...]
    weight = w_ref[...]
    acc_ref[...] += lax.dot_general(rows, weight, (((1,), (1,)), ((), ())), preferred_element_type=jnp.float32)
    part = jnp.dot(acts_ref[...], rows, preferred_element_type=jnp.float32)
    neww_ref[...] = (weight.astype(jnp.float32) - rate * (part * scale)).astype(neww_ref.dtype)

    @pl.when(i == pl.num_programs(0) - 1)
    def _():
        grad_ref[...] = (acc_ref[...] * scale).astype(grad_ref.dtype)


def tail(piece, weight, acts_t, scale, rate, chunk=512):
    rows, width = piece.shape
    share = weight.shape[0]
    return pl.pallas_call(
        functools.partial(tail_kernel, scale=scale, rate=rate),
        grid=(width // chunk,),
        in_specs=[pl.BlockSpec((rows, chunk), lambda i: (0, i)),
                  pl.BlockSpec((share, chunk), lambda i: (0, i)),
                  pl.BlockSpec((share, rows), lambda i: (0, 0))],
        out_specs=[pl.BlockSpec((rows, share), lambda i: (0, 0)),
                   pl.BlockSpec((share, chunk), lambda i: (0, i))],
        out_shape=[jax.ShapeDtypeStruct((rows, share), jnp.bfloat16),
                   jax.ShapeDtypeStruct((share, width), jnp.bfloat16)],
        scratch_shapes=[pltpu.VMEM((rows, share), jnp.float32)],
        compiler_params=pltpu.CompilerParams(dimension_semantics=("arbitrary",)),
    )(piece, weight, acts_t)


def shards(grad_out, hidden, weights, counts):
    row_total = grad_out.shape[3]
    full_width = grad_out.shape[4]
    micro = grad_out.shape[2]
    tokens = hidden.shape[3]
    share = hidden.shape[4]
    scale_factor = float(full_width) ** (-0.5)
    slot_index = lax.broadcasted_iota(jnp.int32, (1, 1, 1, row_total), 3)
    live_rows = slot_index < counts
    masked = jnp.where(live_rows[..., None], grad_out, jnp.zeros_like(grad_out))
    own_weight = weights[0]
    mirror_masked, mirror_hidden = mirror((masked[0, 1], hidden[0, 1]))
    both_masked = jnp.stack([masked[0, 0], mirror_masked], axis=0)
    both_hidden = jnp.stack([hidden[0, 0], mirror_hidden], axis=0)
    piece = gather_rows(both_masked.reshape(-1, full_width))
    ranks = tokens // row_total
    acts = both_hidden.reshape(2, micro, ranks, row_total, share).transpose(2, 0, 1, 3, 4).reshape(-1, share)
    grad, new_weight = tail(piece, own_weight, acts.T, scale_factor, step_rate)
    grad = grad.reshape(ranks, 2, micro, row_total, share).transpose(1, 2, 0, 3, 4).reshape(2, micro, tokens, share)
    returned = mirror(grad[1])
    grad_hidden = jnp.stack([grad[0], returned], axis=0)[None]
    return (grad_hidden, new_weight[None])


def solution(mesh):
    n_pipe, n_dp = mesh.devices.shape
    fine = Mesh(mesh.devices.reshape(4, n_pipe // 4, 4, 4, n_dp // 16), PIPE + DP)
    return jax.shard_map(
        shards,
        mesh=fine,
        in_specs=(
            P(PIPE, None, None, DP, None),
            P(PIPE, None, None, None, DP),
            P(PIPE, DP, None),
            P(PIPE, None, None, DP),
        ),
        out_specs=(P(PIPE, None, None, None, DP), P(PIPE, DP, None)),
        check_vma=False,
    )
```

```python
import jax
import jax.numpy as jnp
from jax import lax
from jax.sharding import Mesh
from jax.sharding import PartitionSpec as P

step_rate = 2.0

PIPE = ("py", "pz")
DP = ("dz", "dx", "dc")


def mirror(block):
    count = lax.axis_size(PIPE)
    route = [(low, count - 1 - low) for low in range(count)]
    return lax.ppermute(block, PIPE, route)


def gather_rows(block):
    half = block.shape[-1] // 2
    out = lax.all_gather(block, "dz", axis=0)
    out = jnp.concatenate(
        [lax.all_gather(out[..., :half], "dx", axis=1), lax.all_gather(out[..., half:], "dx", axis=1)], axis=-1
    )
    other = lax.ppermute(out, "dc", [(0, 1), (1, 0)])
    return jnp.stack([out, other], axis=0)


def own_first(array):
    return jnp.where(lax.axis_index("dc") == 0, array, array[::-1])


def shards(grad_out, hidden, weights, counts):
    row_total = grad_out.shape[3]
    full_width = grad_out.shape[4]
    micro = grad_out.shape[2]
    tokens = hidden.shape[3]
    share = hidden.shape[4]
    n_z, n_x, n_c = (lax.axis_size(name) for name in DP)
    scale_factor = float(full_width) ** (-0.5)
    slot_index = lax.broadcasted_iota(jnp.int32, (1, 1, 1, row_total), 3)
    live_rows = slot_index < counts
    masked = jnp.where(live_rows[..., None], grad_out, jnp.zeros_like(grad_out))
    own_weight = weights[0]
    mirror_masked, mirror_hidden = mirror((masked[0, 1], hidden[0, 1]))
    both_masked = jnp.stack([masked[0, 0], mirror_masked], axis=0)
    both_hidden = jnp.stack([hidden[0, 0], mirror_hidden], axis=0)
    piece = gather_rows(both_masked.reshape(-1, full_width)).reshape(-1, full_width)
    acts = both_hidden.reshape(2, micro, n_z, n_x, n_c, row_total, share).transpose(4, 2, 3, 0, 1, 5, 6)
    acts = own_first(acts).reshape(-1, share)
    grad = jnp.dot(piece, own_weight.T, preferred_element_type=jnp.float32)
    grad = (grad * scale_factor).astype(jnp.bfloat16)
    grad = own_first(grad.reshape(n_c, n_z, n_x, 2, micro, row_total, share))
    grad = grad.transpose(3, 4, 1, 2, 0, 5, 6).reshape(2, micro, tokens, share)
    total = jnp.dot(acts.T, piece, preferred_element_type=jnp.float32)
    gradient = total * scale_factor
    new_weight = (own_weight.astype(jnp.float32) - step_rate * gradient).astype(jnp.bfloat16)
    returned = mirror(grad[1])
    grad_hidden = jnp.stack([grad[0], returned], axis=0)[None]
    return (grad_hidden, new_weight[None])


def solution(mesh):
    n_pipe, n_dp = mesh.devices.shape
    fine = Mesh(mesh.devices.reshape(4, n_pipe // 4, 4, 4, n_dp // 16), PIPE + DP)
    return jax.shard_map(
        shards,
        mesh=fine,
        in_specs=(
            P(PIPE, None, None, DP, None),
            P(PIPE, None, None, None, DP),
            P(PIPE, DP, None),
            P(PIPE, None, None, DP),
        ),
        out_specs=(P(PIPE, None, None, None, DP), P(PIPE, DP, None)),
        check_vma=False,
    )
```

```python
import jax
import jax.numpy as jnp
from jax import lax
from jax.sharding import Mesh
from jax.sharding import PartitionSpec as P

step_rate = 2.0

PIPE = ("py", "pz")
DP = ("dz", "dx", "dc")


def mirror(block):
    count = lax.axis_size(PIPE)
    route = [(low, count - 1 - low) for low in range(count)]
    return lax.ppermute(block, PIPE, route)


def mirror_pair(rows, acts):
    lane = 128
    flat = jnp.concatenate([rows.reshape(-1, lane), acts.reshape(-1, lane)], axis=0)
    flat = mirror(flat)
    split_at = rows.size // lane
    return flat[:split_at].reshape(rows.shape), flat[split_at:].reshape(acts.shape)


def pick_core(array, axis, core):
    return lax.dynamic_index_in_dim(array, core, axis=axis, keepdims=False)


def shards(grad_out, hidden, weights, counts):
    row_total = grad_out.shape[3]
    full_width = grad_out.shape[4]
    micro = grad_out.shape[2]
    tokens = hidden.shape[3]
    share = hidden.shape[4]
    n_z, n_x, n_c = (lax.axis_size(name) for name in DP)
    scale_factor = float(full_width) ** (-0.5)
    slot_index = lax.broadcasted_iota(jnp.int32, (1, 1, 1, row_total), 3)
    live_rows = slot_index < counts
    masked = jnp.where(live_rows[..., None], grad_out, jnp.zeros_like(grad_out))
    own_weight = weights[0]
    mirror_masked, mirror_hidden = mirror_pair(masked[0, 1], hidden[0, 1])
    rows = jnp.stack([masked[0, 0], mirror_masked], axis=0).reshape(2, -1, full_width)
    rows = lax.all_gather(rows, "dz", axis=1)
    core = lax.axis_index("dc")
    cores = (core, n_c - 1 - core)
    grads = []
    total = None
    for slot, acts in enumerate((hidden[0, 0], mirror_hidden)):
        own = lax.all_gather(rows[slot], "dx", axis=1)
        other = lax.ppermute(own, "dc", [(0, 1), (1, 0)])
        acts = acts.reshape(micro, n_z, n_x, n_c, row_total, share)
        parts = []
        for piece, which in zip((own, other), cores):
            piece = piece.reshape(-1, full_width)
            grad = jnp.dot(piece, own_weight.T, preferred_element_type=jnp.float32)
            parts.append((grad * scale_factor).astype(jnp.bfloat16))
            part_acts = pick_core(acts, 3, which).transpose(1, 2, 0, 3, 4).reshape(-1, share)
            part = jnp.dot(part_acts.T, piece, preferred_element_type=jnp.float32)
            total = part if total is None else total + part
        grad = jnp.stack(parts, axis=0).reshape(n_c, n_z, n_x, micro, row_total, share)
        grad = jnp.where(core == 0, grad, grad[::-1])
        grads.append(grad.transpose(3, 1, 2, 0, 4, 5).reshape(micro, tokens, share))
    gradient = total * scale_factor
    new_weight = (own_weight.astype(jnp.float32) - step_rate * gradient).astype(jnp.bfloat16)
    returned = mirror(grads[1])
    grad_hidden = jnp.stack([grads[0], returned], axis=0)[None]
    return (grad_hidden, new_weight[None])


def solution(mesh):
    n_pipe, n_dp = mesh.devices.shape
    fine = Mesh(mesh.devices.reshape(4, n_pipe // 4, 4, 4, n_dp // 16), PIPE + DP)
    return jax.shard_map(
        shards,
        mesh=fine,
        in_specs=(
            P(PIPE, None, None, DP, None),
            P(PIPE, None, None, None, DP),
            P(PIPE, DP, None),
            P(PIPE, None, None, DP),
        ),
        out_specs=(P(PIPE, None, None, None, DP), P(PIPE, DP, None)),
        check_vma=False,
    )
```

```python
import jax
import jax.numpy as jnp
from jax import lax
from jax.sharding import Mesh
from jax.sharding import PartitionSpec as P

step_rate = 2.0

PIPE = ("py", "pz")
DP = ("dz", "dx", "dc")


def mirror(block):
    count = lax.axis_size(PIPE)
    route = [(low, count - 1 - low) for low in range(count)]
    return lax.ppermute(block, PIPE, route)


def mirror_pair(rows, acts):
    lane = 128
    flat = jnp.concatenate([rows.reshape(-1, lane), acts.reshape(-1, lane)], axis=0)
    flat = mirror(flat)
    split_at = rows.size // lane
    return flat[:split_at].reshape(rows.shape), flat[split_at:].reshape(acts.shape)


def gather_rows(block):
    half = block.shape[-1] // 2
    out = lax.all_gather(block, "dz", axis=0)
    out = jnp.concatenate(
        [lax.all_gather(out[..., :half], "dx", axis=1), lax.all_gather(out[..., half:], "dx", axis=1)], axis=-1
    )
    other = lax.ppermute(out, "dc", [(0, 1), (1, 0)])
    return jnp.stack([out, other], axis=0)


def own_first(array):
    return jnp.where(lax.axis_index("dc") == 0, array, array[::-1])


def shards(grad_out, hidden, weights, counts):
    row_total = grad_out.shape[3]
    full_width = grad_out.shape[4]
    micro = grad_out.shape[2]
    tokens = hidden.shape[3]
    share = hidden.shape[4]
    n_z, n_x, n_c = (lax.axis_size(name) for name in DP)
    scale_factor = float(full_width) ** (-0.5)
    slot_index = lax.broadcasted_iota(jnp.int32, (1, 1, 1, row_total), 3)
    live_rows = slot_index < counts
    masked = jnp.where(live_rows[..., None], grad_out, jnp.zeros_like(grad_out))
    own_weight = weights[0]
    mirror_masked, mirror_hidden = mirror_pair(masked[0, 1], hidden[0, 1])
    both_masked = jnp.stack([masked[0, 0], mirror_masked], axis=0)
    both_hidden = jnp.stack([hidden[0, 0], mirror_hidden], axis=0)
    piece = gather_rows(both_masked.reshape(-1, full_width)).reshape(-1, full_width)
    acts = both_hidden.reshape(2, micro, n_z, n_x, n_c, row_total, share).transpose(4, 2, 3, 0, 1, 5, 6)
    acts = own_first(acts).reshape(-1, share)
    grad = jnp.dot(piece, own_weight.T, preferred_element_type=jnp.float32)
    grad = (grad * scale_factor).astype(jnp.bfloat16)
    grad = own_first(grad.reshape(n_c, n_z, n_x, 2, micro, row_total, share))
    grad = grad.transpose(3, 4, 1, 2, 0, 5, 6).reshape(2, micro, tokens, share)
    total = jnp.dot(acts.T, piece, preferred_element_type=jnp.float32)
    gradient = total * scale_factor
    new_weight = (own_weight.astype(jnp.float32) - step_rate * gradient).astype(jnp.bfloat16)
    returned = mirror(grad[1])
    grad_hidden = jnp.stack([grad[0], returned], axis=0)[None]
    return (grad_hidden, new_weight[None])


def solution(mesh):
    n_pipe, n_dp = mesh.devices.shape
    fine = Mesh(mesh.devices.reshape(4, n_pipe // 4, 4, 4, n_dp // 16), PIPE + DP)
    return jax.shard_map(
        shards,
        mesh=fine,
        in_specs=(
            P(PIPE, None, None, DP, None),
            P(PIPE, None, None, None, DP),
            P(PIPE, DP, None),
            P(PIPE, None, None, DP),
        ),
        out_specs=(P(PIPE, None, None, None, DP), P(PIPE, DP, None)),
        check_vma=False,
    )
```

```python
import jax
import jax.numpy as jnp
from jax import lax
from jax.sharding import Mesh
from jax.sharding import PartitionSpec as P

step_rate = 2.0

PIPE = ("py", "pz")
DP = ("dz", "dx", "dc")


def mirror(block):
    count = lax.axis_size(PIPE)
    route = [(low, count - 1 - low) for low in range(count)]
    return lax.ppermute(block, PIPE, route)


def mirror_pair(rows, acts):
    lane = 128
    flat = jnp.concatenate([rows.reshape(-1, lane), acts.reshape(-1, lane)], axis=0)
    flat = mirror(flat)
    split_at = rows.size // lane
    return flat[:split_at].reshape(rows.shape), flat[split_at:].reshape(acts.shape)


def gather_rows(block):
    half = block.shape[-1] // 2
    out = lax.all_gather(block, "dz", axis=0)
    out = jnp.concatenate(
        [lax.all_gather(out[..., :half], "dx", axis=1), lax.all_gather(out[..., half:], "dx", axis=1)], axis=-1
    )
    other = lax.ppermute(out, "dc", [(0, 1), (1, 0)])
    return out, other


def own_first(array):
    return jnp.where(lax.axis_index("dc") == 0, array, array[::-1])


def shards(grad_out, hidden, weights, counts):
    row_total = grad_out.shape[3]
    full_width = grad_out.shape[4]
    micro = grad_out.shape[2]
    tokens = hidden.shape[3]
    share = hidden.shape[4]
    n_z, n_x, n_c = (lax.axis_size(name) for name in DP)
    scale_factor = float(full_width) ** (-0.5)
    slot_index = lax.broadcasted_iota(jnp.int32, (1, 1, 1, row_total), 3)
    live_rows = slot_index < counts
    masked = jnp.where(live_rows[..., None], grad_out, jnp.zeros_like(grad_out))
    own_weight = weights[0]
    mirror_masked, mirror_hidden = mirror_pair(masked[0, 1], hidden[0, 1])
    both_masked = jnp.stack([masked[0, 0], mirror_masked], axis=0)
    both_hidden = jnp.stack([hidden[0, 0], mirror_hidden], axis=0)
    pieces = [piece.reshape(-1, full_width) for piece in gather_rows(both_masked.reshape(-1, full_width))]
    acts = both_hidden.reshape(2, micro, n_z, n_x, n_c, row_total, share).transpose(4, 2, 3, 0, 1, 5, 6)
    acts = own_first(acts).reshape(n_c, -1, share)
    grads = []
    total = None
    for index, piece in enumerate(pieces):
        grad = jnp.dot(piece, own_weight.T, preferred_element_type=jnp.float32)
        grads.append((grad * scale_factor).astype(jnp.bfloat16))
        part = jnp.dot(acts[index].T, piece, preferred_element_type=jnp.float32)
        total = part if total is None else total + part
    grad = own_first(jnp.stack(grads, axis=0).reshape(n_c, n_z, n_x, 2, micro, row_total, share))
    grad = grad.transpose(3, 4, 1, 2, 0, 5, 6).reshape(2, micro, tokens, share)
    gradient = total * scale_factor
    new_weight = (own_weight.astype(jnp.float32) - step_rate * gradient).astype(jnp.bfloat16)
    returned = mirror(grad[1])
    grad_hidden = jnp.stack([grad[0], returned], axis=0)[None]
    return (grad_hidden, new_weight[None])


def solution(mesh):
    n_pipe, n_dp = mesh.devices.shape
    fine = Mesh(mesh.devices.reshape(4, n_pipe // 4, 4, 4, n_dp // 16), PIPE + DP)
    return jax.shard_map(
        shards,
        mesh=fine,
        in_specs=(
            P(PIPE, None, None, DP, None),
            P(PIPE, None, None, None, DP),
            P(PIPE, DP, None),
            P(PIPE, None, None, DP),
        ),
        out_specs=(P(PIPE, None, None, None, DP), P(PIPE, DP, None)),
        check_vma=False,
    )
```

```python
import jax
import jax.numpy as jnp
from jax import lax
from jax.sharding import Mesh
from jax.sharding import PartitionSpec as P

step_rate = 2.0

PIPE = ("py", "pz")
DP = ("dz", "dx", "dc")


def mirror(block):
    count = lax.axis_size(PIPE)
    route = [(low, count - 1 - low) for low in range(count)]
    return lax.ppermute(block, PIPE, route)


def mirror_pair(rows, acts):
    lane = 128
    flat = jnp.concatenate([rows.reshape(-1, lane), acts.reshape(-1, lane)], axis=0)
    flat = mirror(flat)
    split_at = rows.size // lane
    return flat[:split_at].reshape(rows.shape), flat[split_at:].reshape(acts.shape)


def own_first(array):
    return jnp.where(lax.axis_index("dc") == 0, array, array[::-1])


def shards(grad_out, hidden, weights, counts):
    row_total = grad_out.shape[3]
    full_width = grad_out.shape[4]
    micro = grad_out.shape[2]
    tokens = hidden.shape[3]
    share = hidden.shape[4]
    n_z, n_x, n_c = (lax.axis_size(name) for name in DP)
    scale_factor = float(full_width) ** (-0.5)
    slot_index = lax.broadcasted_iota(jnp.int32, (1, 1, 1, row_total), 3)
    live_rows = slot_index < counts
    masked = jnp.where(live_rows[..., None], grad_out, jnp.zeros_like(grad_out))
    own_weight = weights[0]
    own_rows = jnp.stack([masked[0, 0], masked[0, 1]], axis=0).reshape(2, -1, full_width)
    own_rows = lax.all_gather(own_rows, "dz", axis=1)
    mirror_rows, mirror_hidden = mirror_pair(own_rows[1], hidden[0, 1])
    both_rows = jnp.stack(
        [lax.all_gather(own_rows[0], "dx", axis=1), lax.all_gather(mirror_rows, "dx", axis=1)], axis=0
    )
    other_rows = lax.ppermute(both_rows, "dc", [(0, 1), (1, 0)])
    both_hidden = jnp.stack([hidden[0, 0], mirror_hidden], axis=0)
    pieces = [both_rows.reshape(-1, full_width), other_rows.reshape(-1, full_width)]
    acts = both_hidden.reshape(2, micro, n_z, n_x, n_c, row_total, share).transpose(4, 0, 2, 3, 1, 5, 6)
    acts = own_first(acts).reshape(n_c, -1, share)
    grads = []
    total = None
    for index, piece in enumerate(pieces):
        grad = jnp.dot(piece, own_weight.T, preferred_element_type=jnp.float32)
        grads.append((grad * scale_factor).astype(jnp.bfloat16))
        part = jnp.dot(acts[index].T, piece, preferred_element_type=jnp.float32)
        total = part if total is None else total + part
    grad = own_first(jnp.stack(grads, axis=0).reshape(n_c, 2, n_z, n_x, micro, row_total, share))
    grad = grad.transpose(1, 4, 2, 3, 0, 5, 6).reshape(2, micro, tokens, share)
    gradient = total * scale_factor
    new_weight = (own_weight.astype(jnp.float32) - step_rate * gradient).astype(jnp.bfloat16)
    returned = mirror(grad[1])
    grad_hidden = jnp.stack([grad[0], returned], axis=0)[None]
    return (grad_hidden, new_weight[None])


def solution(mesh):
    n_pipe, n_dp = mesh.devices.shape
    fine = Mesh(mesh.devices.reshape(4, n_pipe // 4, 4, 4, n_dp // 16), PIPE + DP)
    return jax.shard_map(
        shards,
        mesh=fine,
        in_specs=(
            P(PIPE, None, None, DP, None),
            P(PIPE, None, None, None, DP),
            P(PIPE, DP, None),
            P(PIPE, None, None, DP),
        ),
        out_specs=(P(PIPE, None, None, None, DP), P(PIPE, DP, None)),
        check_vma=False,
    )
```

```python
import jax
import jax.numpy as jnp
from jax import lax
from jax.sharding import Mesh
from jax.sharding import PartitionSpec as P

step_rate = 2.0

PIPE = ("py", "pz")
DP = ("dz", "dx", "dc")


def mirror(block):
    count = lax.axis_size(PIPE)
    route = [(low, count - 1 - low) for low in range(count)]
    return lax.ppermute(block, PIPE, route)


def mirror_pair(rows, acts):
    lane = 128
    flat = jnp.concatenate([rows.reshape(-1, lane), acts.reshape(-1, lane)], axis=0)
    flat = mirror(flat)
    split_at = rows.size // lane
    return flat[:split_at].reshape(rows.shape), flat[split_at:].reshape(acts.shape)


def own_first(array):
    return jnp.where(lax.axis_index("dc") == 0, array, array[::-1])


def shards(grad_out, hidden, weights, counts):
    row_total = grad_out.shape[3]
    full_width = grad_out.shape[4]
    micro = grad_out.shape[2]
    tokens = hidden.shape[3]
    share = hidden.shape[4]
    n_z, n_x, n_c = (lax.axis_size(name) for name in DP)
    scale_factor = float(full_width) ** (-0.5)
    slot_index = lax.broadcasted_iota(jnp.int32, (1, 1, 1, row_total), 3)
    live_rows = slot_index < counts
    masked = jnp.where(live_rows[..., None], grad_out, jnp.zeros_like(grad_out))
    own_weight = weights[0]
    own_rows = jnp.stack([masked[0, 0], masked[0, 1]], axis=0).reshape(2, -1, full_width)
    own_rows = lax.all_gather(own_rows, "dz", axis=1)
    mirror_rows, mirror_hidden = mirror_pair(own_rows[1], hidden[0, 1])
    both_rows = jnp.stack(
        [lax.all_gather(own_rows[0], "dx", axis=1), lax.all_gather(mirror_rows, "dx", axis=1)], axis=0
    )
    other_rows = lax.ppermute(both_rows, "dc", [(0, 1), (1, 0)])
    both_hidden = jnp.stack([hidden[0, 0], mirror_hidden], axis=0)
    pieces = [both_rows.reshape(-1, full_width), other_rows.reshape(-1, full_width)]
    acts = both_hidden.reshape(2, micro, n_z, n_x, n_c, row_total, share).transpose(4, 0, 2, 3, 1, 5, 6)
    acts = own_first(acts).reshape(n_c, -1, share)
    grads = []
    total = None
    for index, piece in enumerate(pieces):
        grad = [
            jnp.dot(rows, own_weight.T, preferred_element_type=jnp.float32)
            for rows in piece.reshape(2, -1, full_width)[::-1]
        ]
        grads.append((jnp.stack(grad[::-1], axis=0) * scale_factor).astype(jnp.bfloat16))
        part = jnp.dot(acts[index].T, piece, preferred_element_type=jnp.float32)
        total = part if total is None else total + part
    grad = own_first(jnp.stack(grads, axis=0).reshape(n_c, 2, n_z, n_x, micro, row_total, share))
    grad = grad.transpose(1, 4, 2, 3, 0, 5, 6).reshape(2, micro, tokens, share)
    gradient = total * scale_factor
    new_weight = (own_weight.astype(jnp.float32) - step_rate * gradient).astype(jnp.bfloat16)
    returned = mirror(grad[1])
    grad_hidden = jnp.stack([grad[0], returned], axis=0)[None]
    return (grad_hidden, new_weight[None])


def solution(mesh):
    n_pipe, n_dp = mesh.devices.shape
    fine = Mesh(mesh.devices.reshape(4, n_pipe // 4, 4, 4, n_dp // 16), PIPE + DP)
    return jax.shard_map(
        shards,
        mesh=fine,
        in_specs=(
            P(PIPE, None, None, DP, None),
            P(PIPE, None, None, None, DP),
            P(PIPE, DP, None),
            P(PIPE, None, None, DP),
        ),
        out_specs=(P(PIPE, None, None, None, DP), P(PIPE, DP, None)),
        check_vma=False,
    )
```

```python
import jax
import jax.numpy as jnp
from jax import lax
from jax.sharding import Mesh
from jax.sharding import PartitionSpec as P

step_rate = 2.0

PIPE = ("py", "pz")
DP = ("dz", "dx", "dc")


def mirror(block):
    count = lax.axis_size(PIPE)
    route = [(low, count - 1 - low) for low in range(count)]
    return lax.ppermute(block, PIPE, route)


def mirror_pair(rows, acts):
    lane = 128
    flat = jnp.concatenate([rows.reshape(-1, lane), acts.reshape(-1, lane)], axis=0)
    flat = mirror(flat)
    split_at = rows.size // lane
    return flat[:split_at].reshape(rows.shape), flat[split_at:].reshape(acts.shape)


def own_first(array):
    return jnp.where(lax.axis_index("dc") == 0, array, array[::-1])


def shards(grad_out, hidden, weights, counts):
    row_total = grad_out.shape[3]
    full_width = grad_out.shape[4]
    micro = grad_out.shape[2]
    tokens = hidden.shape[3]
    share = hidden.shape[4]
    n_z, n_x, n_c = (lax.axis_size(name) for name in DP)
    scale_factor = float(full_width) ** (-0.5)
    slot_index = lax.broadcasted_iota(jnp.int32, (1, 1, 1, row_total), 3)
    live_rows = slot_index < counts
    masked = jnp.where(live_rows[..., None], grad_out, jnp.zeros_like(grad_out))
    own_weight = weights[0]
    own_rows = jnp.stack([masked[0, 0], masked[0, 1]], axis=0).reshape(2, -1, full_width)
    own_rows = lax.all_gather(own_rows, "dz", axis=1)
    mirror_rows, mirror_hidden = mirror_pair(own_rows[1], jnp.swapaxes(hidden[0, 1], -1, -2))
    mirror_hidden = jnp.swapaxes(mirror_hidden, -1, -2)
    both_rows = jnp.stack(
        [lax.all_gather(own_rows[0], "dx", axis=1), lax.all_gather(mirror_rows, "dx", axis=1)], axis=0
    )
    other_rows = lax.ppermute(both_rows, "dc", [(0, 1), (1, 0)])
    both_hidden = jnp.stack([hidden[0, 0], mirror_hidden], axis=0)
    pieces = [both_rows.reshape(-1, full_width), other_rows.reshape(-1, full_width)]
    acts = both_hidden.reshape(2, micro, n_z, n_x, n_c, row_total, share).transpose(4, 0, 2, 3, 1, 5, 6)
    acts = own_first(acts).reshape(n_c, -1, share)
    grads = []
    total = None
    for index, piece in enumerate(pieces):
        grad = jnp.dot(piece, own_weight.T, preferred_element_type=jnp.float32)
        grads.append((grad * scale_factor).astype(jnp.bfloat16))
        part = jnp.dot(acts[index].T, piece, preferred_element_type=jnp.float32)
        total = part if total is None else total + part
    grad = own_first(jnp.stack(grads, axis=0).reshape(n_c, 2, n_z, n_x, micro, row_total, share))
    grad = grad.transpose(1, 4, 2, 3, 0, 5, 6).reshape(2, micro, tokens, share)
    gradient = total * scale_factor
    new_weight = (own_weight.astype(jnp.float32) - step_rate * gradient).astype(jnp.bfloat16)
    returned = mirror(grad[1])
    grad_hidden = jnp.stack([grad[0], returned], axis=0)[None]
    return (grad_hidden, new_weight[None])


def solution(mesh):
    n_pipe, n_dp = mesh.devices.shape
    fine = Mesh(mesh.devices.reshape(4, n_pipe // 4, 4, 4, n_dp // 16), PIPE + DP)
    return jax.shard_map(
        shards,
        mesh=fine,
        in_specs=(
            P(PIPE, None, None, DP, None),
            P(PIPE, None, None, None, DP),
            P(PIPE, DP, None),
            P(PIPE, None, None, DP),
        ),
        out_specs=(P(PIPE, None, None, None, DP), P(PIPE, DP, None)),
        check_vma=False,
    )
```

```python
import jax
import jax.numpy as jnp
from jax import lax
from jax.sharding import Mesh
from jax.sharding import PartitionSpec as P

step_rate = 2.0

PIPE = ("py", "pz")
DP = ("dz", "dx", "dc")


def mirror(block):
    count = lax.axis_size(PIPE)
    route = [(low, count - 1 - low) for low in range(count)]
    return lax.ppermute(block, PIPE, route)


def mirror_pair(rows, acts):
    lane = 128
    flat = jnp.concatenate([rows.reshape(-1, lane), acts.reshape(-1, lane)], axis=0)
    flat = mirror(flat)
    split_at = rows.size // lane
    return flat[:split_at].reshape(rows.shape), flat[split_at:].reshape(acts.shape)


def own_first(array):
    return jnp.where(lax.axis_index("dc") == 0, array, array[::-1])


def shards(grad_out, hidden, weights, counts):
    row_total = grad_out.shape[3]
    full_width = grad_out.shape[4]
    micro = grad_out.shape[2]
    tokens = hidden.shape[3]
    share = hidden.shape[4]
    n_z, n_x, n_c = (lax.axis_size(name) for name in DP)
    scale_factor = float(full_width) ** (-0.5)
    slot_index = lax.broadcasted_iota(jnp.int32, grad_out.shape, 3)
    masked = jnp.where(slot_index < counts[..., None], grad_out, jnp.zeros_like(grad_out))
    own_weight = weights[0]
    own_rows = jnp.stack([masked[0, 0], masked[0, 1]], axis=0).reshape(2, -1, full_width)
    own_rows = lax.all_gather(own_rows, "dz", axis=1)
    mirror_rows, mirror_hidden = mirror_pair(own_rows[1], jnp.swapaxes(hidden[0, 1], -1, -2))
    mirror_hidden = jnp.swapaxes(mirror_hidden, -1, -2)
    both_rows = jnp.stack(
        [lax.all_gather(own_rows[0], "dx", axis=1), lax.all_gather(mirror_rows, "dx", axis=1)], axis=0
    )
    other_rows = lax.ppermute(both_rows, "dc", [(0, 1), (1, 0)])
    both_hidden = jnp.stack([hidden[0, 0], mirror_hidden], axis=0)
    pieces = [both_rows.reshape(-1, full_width), other_rows.reshape(-1, full_width)]
    acts = both_hidden.reshape(2, micro, n_z, n_x, n_c, row_total, share).transpose(4, 0, 2, 3, 1, 5, 6)
    acts = own_first(acts).reshape(n_c, -1, share)
    grads = []
    total = None
    for index, piece in enumerate(pieces):
        grad = jnp.dot(piece, own_weight.T, preferred_element_type=jnp.float32)
        grads.append((grad * scale_factor).astype(jnp.bfloat16))
        part = jnp.dot(acts[index].T, piece, preferred_element_type=jnp.float32)
        total = part if total is None else total + part
    grad = own_first(jnp.stack(grads, axis=0).reshape(n_c, 2, n_z, n_x, micro, row_total, share))
    grad = grad.transpose(1, 4, 2, 3, 0, 5, 6).reshape(2, micro, tokens, share)
    gradient = total * scale_factor
    new_weight = (own_weight.astype(jnp.float32) - step_rate * gradient).astype(jnp.bfloat16)
    returned = mirror(grad[1])
    grad_hidden = jnp.stack([grad[0], returned], axis=0)[None]
    return (grad_hidden, new_weight[None])


def solution(mesh):
    n_pipe, n_dp = mesh.devices.shape
    fine = Mesh(mesh.devices.reshape(4, n_pipe // 4, 4, 4, n_dp // 16), PIPE + DP)
    return jax.shard_map(
        shards,
        mesh=fine,
        in_specs=(
            P(PIPE, None, None, DP, None),
            P(PIPE, None, None, None, DP),
            P(PIPE, DP, None),
            P(PIPE, None, None, DP),
        ),
        out_specs=(P(PIPE, None, None, None, DP), P(PIPE, DP, None)),
        check_vma=False,
    )
```

```python
import functools

import jax
import jax.numpy as jnp
from jax import lax
from jax.experimental import pallas as pl
from jax.experimental.pallas import tpu as pltpu
from jax.sharding import Mesh
from jax.sharding import PartitionSpec as P

step_rate = 2.0

PIPE = ("py", "pz")
DP = ("dz", "dx", "dc")


def mirror(block):
    count = lax.axis_size(PIPE)
    route = [(low, count - 1 - low) for low in range(count)]
    return lax.ppermute(block, PIPE, route)


def mirror_pair(rows, acts):
    lane = 128
    flat = jnp.concatenate([rows.reshape(-1, lane), acts.reshape(-1, lane)], axis=0)
    flat = mirror(flat)
    split_at = rows.size // lane
    return flat[:split_at].reshape(rows.shape), flat[split_at:].reshape(acts.shape)


def own_first(array):
    return jnp.where(lax.axis_index("dc") == 0, array, array[::-1])


def update_kernel(own_ref, other_ref, acts_ref, weight_ref, out_ref, *, scale, rate):
    part = jnp.dot(acts_ref[0], own_ref[...], preferred_element_type=jnp.float32)
    part = part + jnp.dot(acts_ref[1], other_ref[...], preferred_element_type=jnp.float32)
    out_ref[...] = (weight_ref[...].astype(jnp.float32) - rate * (part * scale)).astype(out_ref.dtype)


def update(own, other, acts_t, weight, scale, rate, chunk=512):
    rows, width = own.shape
    share = weight.shape[0]
    return pl.pallas_call(
        functools.partial(update_kernel, scale=scale, rate=rate),
        grid=(width // chunk,),
        in_specs=[
            pl.BlockSpec((rows, chunk), lambda i: (0, i)),
            pl.BlockSpec((rows, chunk), lambda i: (0, i)),
            pl.BlockSpec((2, share, rows), lambda i: (0, 0, 0)),
            pl.BlockSpec((share, chunk), lambda i: (0, i)),
        ],
        out_specs=pl.BlockSpec((share, chunk), lambda i: (0, i)),
        out_shape=jax.ShapeDtypeStruct((share, width), weight.dtype),
        compiler_params=pltpu.CompilerParams(dimension_semantics=("parallel",)),
    )(own, other, acts_t, weight)


def shards(grad_out, hidden, weights, counts):
    row_total = grad_out.shape[3]
    full_width = grad_out.shape[4]
    micro = grad_out.shape[2]
    tokens = hidden.shape[3]
    share = hidden.shape[4]
    n_z, n_x, n_c = (lax.axis_size(name) for name in DP)
    scale_factor = float(full_width) ** (-0.5)
    slot_index = lax.broadcasted_iota(jnp.int32, grad_out.shape, 3)
    masked = jnp.where(slot_index < counts[..., None], grad_out, jnp.zeros_like(grad_out))
    own_weight = weights[0]
    own_rows = jnp.stack([masked[0, 0], masked[0, 1]], axis=0).reshape(2, -1, full_width)
    own_rows = lax.all_gather(own_rows, "dz", axis=1)
    mirror_rows, mirror_hidden = mirror_pair(own_rows[1], jnp.swapaxes(hidden[0, 1], -1, -2))
    mirror_hidden = jnp.swapaxes(mirror_hidden, -1, -2)
    both_rows = jnp.stack(
        [lax.all_gather(own_rows[0], "dx", axis=1), lax.all_gather(mirror_rows, "dx", axis=1)], axis=0
    )
    other_rows = lax.ppermute(both_rows, "dc", [(0, 1), (1, 0)])
    both_hidden = jnp.stack([hidden[0, 0], mirror_hidden], axis=0)
    pieces = [both_rows.reshape(-1, full_width), other_rows.reshape(-1, full_width)]
    acts = both_hidden.reshape(2, micro, n_z, n_x, n_c, row_total, share).transpose(4, 0, 2, 3, 1, 5, 6)
    acts = own_first(acts).reshape(n_c, -1, share)
    grads = []
    for piece in pieces:
        grad = jnp.dot(piece, own_weight.T, preferred_element_type=jnp.float32)
        grads.append((grad * scale_factor).astype(jnp.bfloat16))
    grad = own_first(jnp.stack(grads, axis=0).reshape(n_c, 2, n_z, n_x, micro, row_total, share))
    grad = grad.transpose(1, 4, 2, 3, 0, 5, 6).reshape(2, micro, tokens, share)
    new_weight = update(pieces[0], pieces[1], jnp.swapaxes(acts, 1, 2), own_weight, scale_factor, step_rate)
    returned = mirror(grad[1])
    grad_hidden = jnp.stack([grad[0], returned], axis=0)[None]
    return (grad_hidden, new_weight[None])


def solution(mesh):
    n_pipe, n_dp = mesh.devices.shape
    fine = Mesh(mesh.devices.reshape(4, n_pipe // 4, 4, 4, n_dp // 16), PIPE + DP)
    return jax.shard_map(
        shards,
        mesh=fine,
        in_specs=(
            P(PIPE, None, None, DP, None),
            P(PIPE, None, None, None, DP),
            P(PIPE, DP, None),
            P(PIPE, None, None, DP),
        ),
        out_specs=(P(PIPE, None, None, None, DP), P(PIPE, DP, None)),
        check_vma=False,
    )
```

```python
import functools

import jax
import jax.numpy as jnp
from jax import lax
from jax.experimental import pallas as pl
from jax.experimental.pallas import tpu as pltpu
from jax.experimental.layout import Layout, with_layout_constraint
from jax.sharding import Mesh
from jax.sharding import PartitionSpec as P

step_rate = 2.0

PIPE = ("py", "pz")
DP = ("dz", "dx", "dc")


def mirror(block):
    count = lax.axis_size(PIPE)
    route = [(low, count - 1 - low) for low in range(count)]
    return lax.ppermute(block, PIPE, route)


def mirror_pair(rows, acts):
    lane = 128
    flat = jnp.concatenate([rows.reshape(-1, lane), acts.reshape(-1, lane)], axis=0)
    flat = mirror(flat)
    split_at = rows.size // lane
    return flat[:split_at].reshape(rows.shape), flat[split_at:].reshape(acts.shape)


def own_first(array):
    return jnp.where(lax.axis_index("dc") == 0, array, array[::-1])


def update_kernel(own_ref, other_ref, acts_ref, weight_ref, out_ref, *, scale, rate):
    part = jnp.dot(acts_ref[0], own_ref[...], preferred_element_type=jnp.float32)
    part = part + jnp.dot(acts_ref[1], other_ref[...], preferred_element_type=jnp.float32)
    out_ref[...] = (weight_ref[...].astype(jnp.float32) - rate * (part * scale)).astype(out_ref.dtype)


def update(own, other, acts_t, weight, scale, rate, chunk=512):
    rows, width = own.shape
    share = weight.shape[0]
    return pl.pallas_call(
        functools.partial(update_kernel, scale=scale, rate=rate),
        grid=(width // chunk,),
        in_specs=[
            pl.BlockSpec((rows, chunk), lambda i: (0, i)),
            pl.BlockSpec((rows, chunk), lambda i: (0, i)),
            pl.BlockSpec((2, share, rows), lambda i: (0, 0, 0)),
            pl.BlockSpec((share, chunk), lambda i: (0, i)),
        ],
        out_specs=pl.BlockSpec((share, chunk), lambda i: (0, i)),
        out_shape=jax.ShapeDtypeStruct((share, width), weight.dtype),
        compiler_params=pltpu.CompilerParams(dimension_semantics=("parallel",)),
    )(own, other, acts_t, weight)


def shards(grad_out, hidden, weights, counts):
    row_total = grad_out.shape[3]
    full_width = grad_out.shape[4]
    micro = grad_out.shape[2]
    tokens = hidden.shape[3]
    share = hidden.shape[4]
    n_z, n_x, n_c = (lax.axis_size(name) for name in DP)
    scale_factor = float(full_width) ** (-0.5)
    slot_index = lax.broadcasted_iota(jnp.int32, grad_out.shape, 3)
    masked = jnp.where(slot_index < counts[..., None], grad_out, jnp.zeros_like(grad_out))
    own_weight = weights[0]
    own_rows = jnp.stack([masked[0, 0], masked[0, 1]], axis=0).reshape(2, -1, full_width)
    own_rows = lax.all_gather(own_rows, "dz", axis=1)
    mirror_rows, mirror_hidden = mirror_pair(own_rows[1], jnp.swapaxes(hidden[0, 1], -1, -2))
    mirror_hidden = jnp.swapaxes(mirror_hidden, -1, -2)
    both_rows = jnp.stack(
        [lax.all_gather(own_rows[0], "dx", axis=1), lax.all_gather(mirror_rows, "dx", axis=1)], axis=0
    )
    other_rows = lax.ppermute(both_rows, "dc", [(0, 1), (1, 0)])
    both_hidden = jnp.stack([hidden[0, 0], mirror_hidden], axis=0)
    pieces = [both_rows.reshape(-1, full_width), other_rows.reshape(-1, full_width)]
    acts = both_hidden.reshape(2, micro, n_z, n_x, n_c, row_total, share).transpose(4, 0, 2, 3, 1, 5, 6)
    acts = own_first(acts).reshape(n_c, -1, share)
    grads = []
    for piece in pieces:
        grad = jnp.dot(piece, own_weight.T, preferred_element_type=jnp.float32)
        grads.append((grad * scale_factor).astype(jnp.bfloat16))
    grad = own_first(jnp.stack(grads, axis=0).reshape(n_c, 2, n_z, n_x, micro, row_total, share))
    grad = grad.transpose(1, 4, 2, 3, 0, 5, 6).reshape(2, micro, tokens, share)
    new_weight = update(pieces[0], pieces[1], jnp.swapaxes(acts, 1, 2), own_weight, scale_factor, step_rate)
    returned = mirror(grad[1])
    grad_hidden = jnp.stack([grad[0], returned], axis=0)[None]
    grad_hidden = with_layout_constraint(grad_hidden, Layout(major_to_minor=(0, 1, 2, 4, 3)))
    return (grad_hidden, new_weight[None])


def solution(mesh):
    n_pipe, n_dp = mesh.devices.shape
    fine = Mesh(mesh.devices.reshape(4, n_pipe // 4, 4, 4, n_dp // 16), PIPE + DP)
    return jax.shard_map(
        shards,
        mesh=fine,
        in_specs=(
            P(PIPE, None, None, DP, None),
            P(PIPE, None, None, None, DP),
            P(PIPE, DP, None),
            P(PIPE, None, None, DP),
        ),
        out_specs=(P(PIPE, None, None, None, DP), P(PIPE, DP, None)),
        check_vma=False,
    )
```

```python
import functools

import jax
import jax.numpy as jnp
from jax import lax
from jax.experimental import pallas as pl
from jax.experimental.pallas import tpu as pltpu
from jax.experimental.layout import Layout, with_layout_constraint
from jax.sharding import Mesh
from jax.sharding import PartitionSpec as P

step_rate = 2.0

PIPE = ("py", "pz")
DP = ("dz", "dx", "dc")


def mirror(block):
    count = lax.axis_size(PIPE)
    route = [(low, count - 1 - low) for low in range(count)]
    return lax.ppermute(block, PIPE, route)


def mirror_pair(rows, acts):
    lane = 128
    flat = jnp.concatenate([rows.reshape(-1, lane), acts.reshape(-1, lane)], axis=0)
    flat = mirror(flat)
    split_at = rows.size // lane
    return flat[:split_at].reshape(rows.shape), flat[split_at:].reshape(acts.shape)


def own_first(array):
    return jnp.where(lax.axis_index("dc") == 0, array, array[::-1])


def update_kernel(own_ref, other_ref, acts_ref, weight_ref, out_ref, *, scale, rate):
    rows_first = (((0,), (0,)), ((), ()))
    part = lax.dot_general(acts_ref[0], own_ref[...], rows_first, preferred_element_type=jnp.float32)
    part = part + lax.dot_general(acts_ref[1], other_ref[...], rows_first, preferred_element_type=jnp.float32)
    out_ref[...] = (weight_ref[...].astype(jnp.float32) - rate * (part * scale)).astype(out_ref.dtype)


def update(own, other, acts, weight, scale, rate, chunk=896):
    rows, width = own.shape
    share = weight.shape[0]
    return pl.pallas_call(
        functools.partial(update_kernel, scale=scale, rate=rate),
        grid=(width // chunk,),
        in_specs=[
            pl.BlockSpec((rows, chunk), lambda i: (0, i)),
            pl.BlockSpec((rows, chunk), lambda i: (0, i)),
            pl.BlockSpec((2, rows, share), lambda i: (0, 0, 0)),
            pl.BlockSpec((share, chunk), lambda i: (0, i)),
        ],
        out_specs=pl.BlockSpec((share, chunk), lambda i: (0, i)),
        out_shape=jax.ShapeDtypeStruct((share, width), weight.dtype),
        compiler_params=pltpu.CompilerParams(dimension_semantics=("parallel",)),
    )(own, other, acts, weight)


def shards(grad_out, hidden, weights, counts):
    row_total = grad_out.shape[3]
    full_width = grad_out.shape[4]
    micro = grad_out.shape[2]
    tokens = hidden.shape[3]
    share = hidden.shape[4]
    n_z, n_x, n_c = (lax.axis_size(name) for name in DP)
    scale_factor = float(full_width) ** (-0.5)
    slot_index = lax.broadcasted_iota(jnp.int32, grad_out.shape, 3)
    masked = jnp.where(slot_index < counts[..., None], grad_out, jnp.zeros_like(grad_out))
    own_weight = weights[0]
    own_rows = jnp.stack([masked[0, 0], masked[0, 1]], axis=0).reshape(2, -1, full_width)
    own_rows = lax.all_gather(own_rows, "dz", axis=1)
    mirror_rows, mirror_hidden = mirror_pair(own_rows[1], jnp.swapaxes(hidden[0, 1], -1, -2))
    mirror_hidden = jnp.swapaxes(mirror_hidden, -1, -2)
    both_rows = jnp.stack(
        [lax.all_gather(own_rows[0], "dx", axis=1), lax.all_gather(mirror_rows, "dx", axis=1)], axis=0
    )
    other_rows = lax.ppermute(both_rows, "dc", [(0, 1), (1, 0)])
    both_hidden = jnp.stack([hidden[0, 0], mirror_hidden], axis=0)
    pieces = [both_rows.reshape(-1, full_width), other_rows.reshape(-1, full_width)]
    acts = both_hidden.reshape(2, micro, n_z, n_x, n_c, row_total, share).transpose(4, 0, 2, 3, 1, 5, 6)
    acts = own_first(acts).reshape(n_c, -1, share)
    grads = []
    for piece in pieces:
        grad = jnp.dot(piece, own_weight.T, preferred_element_type=jnp.float32)
        grads.append((grad * scale_factor).astype(jnp.bfloat16))
    grad = own_first(jnp.stack(grads, axis=0).reshape(n_c, 2, n_z, n_x, micro, row_total, share))
    grad = grad.transpose(1, 4, 2, 3, 0, 5, 6).reshape(2, micro, tokens, share)
    new_weight = update(pieces[0], pieces[1], acts, own_weight, scale_factor, step_rate)
    returned = mirror(grad[1])
    grad_hidden = jnp.stack([grad[0], returned], axis=0)[None]
    grad_hidden = with_layout_constraint(grad_hidden, Layout(major_to_minor=(0, 1, 2, 4, 3)))
    return (grad_hidden, new_weight[None])


def solution(mesh):
    n_pipe, n_dp = mesh.devices.shape
    fine = Mesh(mesh.devices.reshape(4, n_pipe // 4, 4, 4, n_dp // 16), PIPE + DP)
    return jax.shard_map(
        shards,
        mesh=fine,
        in_specs=(
            P(PIPE, None, None, DP, None),
            P(PIPE, None, None, None, DP),
            P(PIPE, DP, None),
            P(PIPE, None, None, DP),
        ),
        out_specs=(P(PIPE, None, None, None, DP), P(PIPE, DP, None)),
        check_vma=False,
    )
```

```python
import functools

import jax
import jax.numpy as jnp
from jax import lax
from jax.experimental import pallas as pl
from jax.experimental.pallas import tpu as pltpu
from jax.experimental.layout import Layout, with_layout_constraint
from jax.sharding import Mesh
from jax.sharding import PartitionSpec as P

step_rate = 2.0

PIPE = ("py", "pz")
DP = ("dz", "dx", "dc")


def mirror(block):
    count = lax.axis_size(PIPE)
    route = [(low, count - 1 - low) for low in range(count)]
    return lax.ppermute(block, PIPE, route)


def mirror_pair(rows, acts):
    lane = 128
    flat = jnp.concatenate([rows.reshape(-1, lane), acts.reshape(-1, lane)], axis=0)
    flat = mirror(flat)
    split_at = rows.size // lane
    return flat[:split_at].reshape(rows.shape), flat[split_at:].reshape(acts.shape)


def own_first(array):
    return jnp.where(lax.axis_index("dc") == 0, array, array[::-1])


def update_kernel(own_ref, other_ref, acts_ref, weight_ref, out_ref, *, scale, rate):
    rows_first = (((0,), (0,)), ((), ()))
    part = lax.dot_general(acts_ref[0], own_ref[...], rows_first, preferred_element_type=jnp.float32)
    part = part + lax.dot_general(acts_ref[1], other_ref[...], rows_first, preferred_element_type=jnp.float32)
    out_ref[...] = (weight_ref[...].astype(jnp.float32) - rate * (part * scale)).astype(out_ref.dtype)


def update(own, other, acts, weight, scale, rate, chunk=896):
    rows, width = own.shape
    share = weight.shape[0]
    return pl.pallas_call(
        functools.partial(update_kernel, scale=scale, rate=rate),
        grid=(width // chunk,),
        in_specs=[
            pl.BlockSpec((rows, chunk), lambda i: (0, i)),
            pl.BlockSpec((rows, chunk), lambda i: (0, i)),
            pl.BlockSpec((2, rows, share), lambda i: (0, 0, 0)),
            pl.BlockSpec((share, chunk), lambda i: (0, i)),
        ],
        out_specs=pl.BlockSpec((share, chunk), lambda i: (0, i)),
        out_shape=jax.ShapeDtypeStruct((share, width), weight.dtype),
        compiler_params=pltpu.CompilerParams(dimension_semantics=("parallel",)),
    )(own, other, acts, weight)


def grad_kernel(rows_ref, weight_ref, out_ref, acc_ref, *, scale):
    step = pl.program_id(0)

    @pl.when(step == 0)
    def _():
        acc_ref[...] = jnp.zeros_like(acc_ref)

    acc_ref[...] += lax.dot_general(
        rows_ref[...], weight_ref[...], (((1,), (1,)), ((), ())), preferred_element_type=jnp.float32
    )

    @pl.when(step == pl.num_programs(0) - 1)
    def _():
        out_ref[...] = (acc_ref[...] * scale).astype(out_ref.dtype)


def row_grad(rows, weight, scale, chunk=896):
    count, width = rows.shape
    share = weight.shape[0]
    return pl.pallas_call(
        functools.partial(grad_kernel, scale=scale),
        grid=(width // chunk,),
        in_specs=[pl.BlockSpec((count, chunk), lambda i: (0, i)), pl.BlockSpec((share, chunk), lambda i: (0, i))],
        out_specs=pl.BlockSpec((count, share), lambda i: (0, 0)),
        out_shape=jax.ShapeDtypeStruct((count, share), rows.dtype),
        scratch_shapes=[pltpu.VMEM((count, share), jnp.float32)],
        compiler_params=pltpu.CompilerParams(dimension_semantics=("arbitrary",)),
    )(rows, weight)


def shards(grad_out, hidden, weights, counts):
    row_total = grad_out.shape[3]
    full_width = grad_out.shape[4]
    micro = grad_out.shape[2]
    tokens = hidden.shape[3]
    share = hidden.shape[4]
    n_z, n_x, n_c = (lax.axis_size(name) for name in DP)
    scale_factor = float(full_width) ** (-0.5)
    slot_index = lax.broadcasted_iota(jnp.int32, grad_out.shape, 3)
    masked = jnp.where(slot_index < counts[..., None], grad_out, jnp.zeros_like(grad_out))
    own_weight = weights[0]
    own_rows = jnp.stack([masked[0, 0], masked[0, 1]], axis=0).reshape(2, -1, full_width)
    own_rows = lax.all_gather(own_rows, "dz", axis=1)
    mirror_rows, mirror_hidden = mirror_pair(own_rows[1], jnp.swapaxes(hidden[0, 1], -1, -2))
    mirror_hidden = jnp.swapaxes(mirror_hidden, -1, -2)
    both_rows = jnp.stack(
        [lax.all_gather(own_rows[0], "dx", axis=1), lax.all_gather(mirror_rows, "dx", axis=1)], axis=0
    )
    other_rows = lax.ppermute(both_rows, "dc", [(0, 1), (1, 0)])
    both_hidden = jnp.stack([hidden[0, 0], mirror_hidden], axis=0)
    pieces = [both_rows.reshape(-1, full_width), other_rows.reshape(-1, full_width)]
    acts = both_hidden.reshape(2, micro, n_z, n_x, n_c, row_total, share).transpose(4, 0, 2, 3, 1, 5, 6)
    acts = own_first(acts).reshape(n_c, -1, share)
    grads = [row_grad(piece, own_weight, scale_factor) for piece in pieces]
    grad = own_first(jnp.stack(grads, axis=0).reshape(n_c, 2, n_z, n_x, micro, row_total, share))
    grad = grad.transpose(1, 4, 2, 3, 0, 5, 6).reshape(2, micro, tokens, share)
    new_weight = update(pieces[0], pieces[1], acts, own_weight, scale_factor, step_rate)
    returned = mirror(grad[1])
    grad_hidden = jnp.stack([grad[0], returned], axis=0)[None]
    grad_hidden = with_layout_constraint(grad_hidden, Layout(major_to_minor=(0, 1, 2, 4, 3)))
    return (grad_hidden, new_weight[None])


def solution(mesh):
    n_pipe, n_dp = mesh.devices.shape
    fine = Mesh(mesh.devices.reshape(4, n_pipe // 4, 4, 4, n_dp // 16), PIPE + DP)
    return jax.shard_map(
        shards,
        mesh=fine,
        in_specs=(
            P(PIPE, None, None, DP, None),
            P(PIPE, None, None, None, DP),
            P(PIPE, DP, None),
            P(PIPE, None, None, DP),
        ),
        out_specs=(P(PIPE, None, None, None, DP), P(PIPE, DP, None)),
        check_vma=False,
    )
```

```python
import functools

import jax
import jax.numpy as jnp
from jax import lax
from jax.experimental import pallas as pl
from jax.experimental.pallas import tpu as pltpu
from jax.experimental.layout import Layout, with_layout_constraint
from jax.sharding import Mesh
from jax.sharding import PartitionSpec as P

step_rate = 2.0

PIPE = ("py", "pz")
DP = ("dz", "dx", "dc")


def mirror(block):
    count = lax.axis_size(PIPE)
    route = [(low, count - 1 - low) for low in range(count)]
    return lax.ppermute(block, PIPE, route)


def mirror_pair(rows, acts):
    lane = 128
    flat = jnp.concatenate([rows.reshape(-1, lane), acts.reshape(-1, lane)], axis=0)
    flat = mirror(flat)
    split_at = rows.size // lane
    return flat[:split_at].reshape(rows.shape), flat[split_at:].reshape(acts.shape)


def own_first(array):
    return jnp.where(lax.axis_index("dc") == 0, array, array[::-1])


def update_kernel(own_ref, other_ref, acts_ref, weight_ref, out_ref, *, scale, rate):
    rows_first = (((0,), (0,)), ((), ()))
    part = lax.dot_general(acts_ref[0], own_ref[...], rows_first, preferred_element_type=jnp.float32)
    part = part + lax.dot_general(acts_ref[1], other_ref[...], rows_first, preferred_element_type=jnp.float32)
    out_ref[...] = (weight_ref[...].astype(jnp.float32) - rate * (part * scale)).astype(out_ref.dtype)


def update(own, other, acts, weight, scale, rate, chunk=896):
    rows, width = own.shape
    share = weight.shape[0]
    return pl.pallas_call(
        functools.partial(update_kernel, scale=scale, rate=rate),
        grid=(width // chunk,),
        in_specs=[
            pl.BlockSpec((rows, chunk), lambda i: (0, i)),
            pl.BlockSpec((rows, chunk), lambda i: (0, i)),
            pl.BlockSpec((2, rows, share), lambda i: (0, 0, 0)),
            pl.BlockSpec((share, chunk), lambda i: (0, i)),
        ],
        out_specs=pl.BlockSpec((share, chunk), lambda i: (0, i)),
        out_shape=jax.ShapeDtypeStruct((share, width), weight.dtype),
        compiler_params=pltpu.CompilerParams(dimension_semantics=("parallel",)),
    )(own, other, acts, weight)


def shards(grad_out, hidden, weights, counts):
    row_total = grad_out.shape[3]
    full_width = grad_out.shape[4]
    micro = grad_out.shape[2]
    tokens = hidden.shape[3]
    share = hidden.shape[4]
    n_z, n_x, n_c = (lax.axis_size(name) for name in DP)
    scale_factor = float(full_width) ** (-0.5)
    slot_index = lax.broadcasted_iota(jnp.int32, grad_out.shape, 3)
    masked = jnp.where(slot_index < counts[..., None], grad_out, jnp.zeros_like(grad_out))
    own_weight = weights[0]
    own_rows = jnp.stack([masked[0, 0], masked[0, 1]], axis=0).reshape(2, -1, full_width)
    own_rows = lax.all_gather(own_rows, "dz", axis=1)
    mirror_rows, mirror_hidden = mirror_pair(own_rows[1], jnp.swapaxes(hidden[0, 1], -1, -2))
    mirror_hidden = jnp.swapaxes(mirror_hidden, -1, -2)
    slot_rows = [lax.all_gather(own_rows[0], "dx", axis=1), lax.all_gather(mirror_rows, "dx", axis=1)]
    other_rows = jnp.stack([lax.ppermute(rows, "dc", [(0, 1), (1, 0)]) for rows in slot_rows], axis=0)
    both_rows = jnp.stack(slot_rows, axis=0)
    both_hidden = jnp.stack([hidden[0, 0], mirror_hidden], axis=0)
    pieces = [both_rows.reshape(-1, full_width), other_rows.reshape(-1, full_width)]
    acts = both_hidden.reshape(2, micro, n_z, n_x, n_c, row_total, share).transpose(4, 0, 2, 3, 1, 5, 6)
    acts = own_first(acts).reshape(n_c, -1, share)
    grads = []
    for piece in pieces:
        grad = jnp.dot(piece, own_weight.T, preferred_element_type=jnp.float32)
        grads.append((grad * scale_factor).astype(jnp.bfloat16))
    grad = own_first(jnp.stack(grads, axis=0).reshape(n_c, 2, n_z, n_x, micro, row_total, share))
    grad = grad.transpose(1, 4, 2, 3, 0, 5, 6).reshape(2, micro, tokens, share)
    new_weight = update(pieces[0], pieces[1], acts, own_weight, scale_factor, step_rate)
    returned = mirror(grad[1])
    grad_hidden = jnp.stack([grad[0], returned], axis=0)[None]
    grad_hidden = with_layout_constraint(grad_hidden, Layout(major_to_minor=(0, 1, 2, 4, 3)))
    return (grad_hidden, new_weight[None])


def solution(mesh):
    n_pipe, n_dp = mesh.devices.shape
    fine = Mesh(mesh.devices.reshape(4, n_pipe // 4, 4, 4, n_dp // 16), PIPE + DP)
    return jax.shard_map(
        shards,
        mesh=fine,
        in_specs=(
            P(PIPE, None, None, DP, None),
            P(PIPE, None, None, None, DP),
            P(PIPE, DP, None),
            P(PIPE, None, None, DP),
        ),
        out_specs=(P(PIPE, None, None, None, DP), P(PIPE, DP, None)),
        check_vma=False,
    )
```

```python
import functools

import jax
import jax.numpy as jnp
from jax import lax
from jax.experimental import pallas as pl
from jax.experimental.pallas import tpu as pltpu
from jax.experimental.layout import Layout, with_layout_constraint
from jax.sharding import Mesh
from jax.sharding import PartitionSpec as P

step_rate = 2.0

PIPE = ("py", "pz")
DP = ("dz", "dx", "dc")


def mirror(block):
    count = lax.axis_size(PIPE)
    route = [(low, count - 1 - low) for low in range(count)]
    return lax.ppermute(block, PIPE, route)


def mirror_pair(rows, acts):
    lane = 128
    flat = jnp.concatenate([rows.reshape(-1, lane), acts.reshape(-1, lane)], axis=0)
    flat = mirror(flat)
    split_at = rows.size // lane
    return flat[:split_at].reshape(rows.shape), flat[split_at:].reshape(acts.shape)


def own_first(array):
    return jnp.where(lax.axis_index("dc") == 0, array, array[::-1])


def update_kernel(own_ref, other_ref, acts_ref, weight_ref, out_ref, *, scale, rate):
    rows_first = (((0,), (0,)), ((), ()))
    part = lax.dot_general(acts_ref[0], own_ref[...], rows_first, preferred_element_type=jnp.float32)
    part = part + lax.dot_general(acts_ref[1], other_ref[...], rows_first, preferred_element_type=jnp.float32)
    out_ref[...] = (weight_ref[...].astype(jnp.float32) - rate * (part * scale)).astype(out_ref.dtype)


def update(own, other, acts, weight, scale, rate, chunk=896):
    rows, width = own.shape
    share = weight.shape[0]
    return pl.pallas_call(
        functools.partial(update_kernel, scale=scale, rate=rate),
        grid=(width // chunk,),
        in_specs=[
            pl.BlockSpec((rows, chunk), lambda i: (0, i)),
            pl.BlockSpec((rows, chunk), lambda i: (0, i)),
            pl.BlockSpec((2, rows, share), lambda i: (0, 0, 0)),
            pl.BlockSpec((share, chunk), lambda i: (0, i)),
        ],
        out_specs=pl.BlockSpec((share, chunk), lambda i: (0, i)),
        out_shape=jax.ShapeDtypeStruct((share, width), weight.dtype),
        compiler_params=pltpu.CompilerParams(dimension_semantics=("parallel",)),
    )(own, other, acts, weight)


def shards(grad_out, hidden, weights, counts):
    row_total = grad_out.shape[3]
    full_width = grad_out.shape[4]
    micro = grad_out.shape[2]
    tokens = hidden.shape[3]
    share = hidden.shape[4]
    n_z, n_x, n_c = (lax.axis_size(name) for name in DP)
    scale_factor = float(full_width) ** (-0.5)
    slot_index = lax.broadcasted_iota(jnp.int32, grad_out.shape, 3)
    masked = jnp.where(slot_index < counts[..., None], grad_out, jnp.zeros_like(grad_out))
    own_weight = weights[0]
    own_rows = jnp.stack([masked[0, 0], masked[0, 1]], axis=0).reshape(2, -1, full_width)
    own_rows = lax.all_gather(own_rows, "dz", axis=1)
    mirror_rows, mirror_hidden = mirror_pair(own_rows[1], jnp.swapaxes(hidden[0, 1], -1, -2))
    mirror_hidden = jnp.swapaxes(mirror_hidden, -1, -2)
    both_rows = jnp.stack(
        [lax.all_gather(own_rows[0], "dx", axis=1), lax.all_gather(mirror_rows, "dx", axis=1)], axis=0
    )
    other_rows = lax.ppermute(both_rows, "dc", [(0, 1), (1, 0)])
    both_hidden = hidden[0].at[1].set(mirror_hidden)
    pieces = [both_rows.reshape(-1, full_width), other_rows.reshape(-1, full_width)]
    acts = both_hidden.reshape(2, micro, n_z, n_x, n_c, row_total, share).transpose(4, 0, 2, 3, 1, 5, 6)
    acts = own_first(acts).reshape(n_c, -1, share)
    grads = []
    for piece in pieces:
        grad = jnp.dot(piece, own_weight.T, preferred_element_type=jnp.float32)
        grads.append((grad * scale_factor).astype(jnp.bfloat16))
    grad = own_first(jnp.stack(grads, axis=0).reshape(n_c, 2, n_z, n_x, micro, row_total, share))
    grad = grad.transpose(1, 4, 2, 3, 0, 5, 6).reshape(2, micro, tokens, share)
    new_weight = update(pieces[0], pieces[1], acts, own_weight, scale_factor, step_rate)
    returned = mirror(grad[1])
    grad_hidden = jnp.stack([grad[0], returned], axis=0)[None]
    grad_hidden = with_layout_constraint(grad_hidden, Layout(major_to_minor=(0, 1, 2, 4, 3)))
    return (grad_hidden, new_weight[None])


def solution(mesh):
    n_pipe, n_dp = mesh.devices.shape
    fine = Mesh(mesh.devices.reshape(4, n_pipe // 4, 4, 4, n_dp // 16), PIPE + DP)
    return jax.shard_map(
        shards,
        mesh=fine,
        in_specs=(
            P(PIPE, None, None, DP, None),
            P(PIPE, None, None, None, DP),
            P(PIPE, DP, None),
            P(PIPE, None, None, DP),
        ),
        out_specs=(P(PIPE, None, None, None, DP), P(PIPE, DP, None)),
        check_vma=False,
    )
```
